32 devices in a mesh: leaf: 8 (over z, x), rhs: 4 (over y, core).
Axes of the slice: x: 2, y: 2, z: 4, core: 2. Of those that a mesh axis runs over, the one named last changes fastest.
Arguments:
- rhs_block: bfloat16 [256, 16384], P('rhs', 'leaf'), may hold values from -6 to 6
- leaf_basis: bfloat16 [16384, 128], P('leaf'), may hold values from -0.5 to 0.5
- local_transfer: bfloat16 [8, 30, 128, 128], P('leaf'), may hold values from -0.375 to 0.375
- top_transfer: bfloat16 [8, 128, 128], replicated, may hold values from -0.375 to 0.375
- coupling_tiles: bfloat16 [64, 128, 128], P('rhs'), may hold values from -0.1875 to 0.1875
- send_index: int32 [8, 8, 4], replicated, may hold values from -1 to 15, as said below
- leaf_list: int32 [2, 128, 192], P(None, 'leaf'), may hold values from 0 to 63, as said below
- top_list: int32 [3, 64], replicated, may hold values from 0 to 63, as said below
Outputs:
- far_field: bfloat16 [256, 16384], P('rhs', 'leaf')
The draws below stay inside these ranges and needn't reach their ends.
Inputs may be any that keep to these rules, and one draw needn't show every extreme that they name: `send_index`: each slot holds a distinct local leaf of the sender or -1; the used slots of a pair come first and the rest are -1; every device fills all 4 slots to itself. `leaf_list`: every slot named in [0] holds a leaf (not -1) for the receiving device that owns the target leaf. `top_list`: target and source lie on the same level of the top tree, at least level 2, and differ by two or more places cyclically within it.
All inputs are finite; a program needn't handle non-finite values.
Results may differ from the reference program's by a relative error of at most 0.017.
Values may be sent and summed in bfloat16 or wider, within the bound.
A program may use at most 192 MiB of HBM per device.

```python
import jax
import jax.numpy as jnp
from jax import lax

RANK = 128
R = 256
M = 128
LOG_LD = 4
C = 4
ENT = 192
TILES = 64
LD = 16
LEAVES = 128
NPTS = 16384
TOPE = 64
N_LEAF = 8


def common_lists(key):
    base = jax.random.fold_in(key, 7301)
    key_count = jax.random.fold_in(base, 1)
    key_perm = jax.random.fold_in(base, 2)
    key_pick = jax.random.fold_in(base, 3)
    key_tile = jax.random.fold_in(base, 4)
    counts = jax.random.randint(key_count, (N_LEAF, N_LEAF), 0, C + 1)
    diag = jnp.arange(N_LEAF)[:, None] == jnp.arange(N_LEAF)[None, :]
    counts = jnp.where(diag, C, counts).astype(jnp.int32)
    keys = jax.random.split(key_perm, N_LEAF * N_LEAF)
    perms = jax.vmap(lambda k: jax.random.permutation(k, LD))(keys).reshape(N_LEAF, N_LEAF, LD)[:, :, :C]
    used = jnp.arange(C)[None, None, :] < counts[:, :, None]
    sends = jnp.where(used, perms, -1).astype(jnp.int32)
    live = jnp.transpose(used, (1, 0, 2)).reshape(N_LEAF, N_LEAF * C).astype(jnp.int32)
    total = jnp.sum(live, axis=1)
    picks = jax.random.randint(key_pick, (N_LEAF, LD * ENT), 0, total[:, None])
    running = jnp.cumsum(live, axis=1)
    slots = jax.vmap(lambda row, want: jnp.searchsorted(row, want + 1, side='left'))(running, picks)
    slots = slots.reshape(LEAVES, ENT).astype(jnp.int32)
    tiles = jax.random.randint(key_tile, (LEAVES, ENT), 0, TILES).astype(jnp.int32)
    return (sends, jnp.stack([slots, tiles]))


def draw_send_index(key, part):
    return common_lists(key)[0]


def draw_leaf_list(key, part):
    return common_lists(key)[1]


def draw_top_list(key, part):
    base = jax.random.fold_in(key, 9113)
    target = jax.random.randint(jax.random.fold_in(base, 1), (TOPE,), 4, 2 * N_LEAF)
    start = jnp.full((TOPE,), 4, jnp.int32)
    power = 8
    while power <= N_LEAF:
        start = jnp.where(target >= power, power, start)
        power = power * 2
    extra = jax.random.randint(jax.random.fold_in(base, 2), (TOPE,), 0, start - 3)
    source = start + (target - start + 2 + extra) % start
    tile = jax.random.randint(jax.random.fold_in(base, 3), (TOPE,), 0, TILES)
    return jnp.stack([target, source, tile]).astype(jnp.int32)


def block_scale(stream_key, extent, shards, smallest, largest):
    loudness = 1.0
    for dim, shards_of in shards:
        steps = jax.random.uniform(jax.random.fold_in(jax.random.fold_in(stream_key, 6), dim), (shards_of,), jnp.float32, smallest / len(shards), largest / len(shards))
        loudness = loudness * jnp.repeat(jnp.exp(steps), extent[dim] // shards_of).reshape((-1,) + (1,) * (len(extent) - 1 - dim))
    return loudness


def scatter_about(stream_key, shape, spread, bound, shards=(), held_as=jnp.bfloat16):
    drawn = jax.random.normal(stream_key, shape, jnp.float32) * spread
    if len(shards) > 0:
        drawn = block_scale(stream_key, shape, shards, -0.22, 0.18) * drawn
    return jnp.clip(drawn, min=-bound, max=bound).astype(held_as)


def setup_inputs(seed: int = 0) -> dict:
    key_of = jax.random.split(jax.random.key(seed), 9)
    rhs_block = scatter_about(key_of[0], (R, NPTS), 1.0, 6.0, ((0, 4), (1, 8)))
    leaf_basis = scatter_about(key_of[1], (NPTS, RANK), M ** -0.5, 0.5, ((0, 8),))
    local_transfer = scatter_about(key_of[2], (N_LEAF, 2 * LD - 2, RANK, RANK), (2 * RANK) ** -0.5, 0.375, ((0, 8),))
    top_transfer = scatter_about(key_of[3], (2 * N_LEAF - 8, RANK, RANK), (2 * RANK) ** -0.5, 0.375)
    coupling_tiles = scatter_about(key_of[4], (TILES, RANK, RANK), (8 * RANK) ** -0.5, 0.1875, ((0, 4),))
    send_index = draw_send_index(jax.random.fold_in(key_of[8], 71), 0)
    leaf_list = draw_leaf_list(jax.random.fold_in(key_of[8], 71), 0)
    top_list = draw_top_list(jax.random.fold_in(key_of[8], 71), 0)
    return dict(rhs_block=rhs_block, leaf_basis=leaf_basis, local_transfer=local_transfer, top_transfer=top_transfer, coupling_tiles=coupling_tiles, send_index=send_index, leaf_list=leaf_list, top_list=top_list)


def reference(rhs_block, leaf_basis, local_transfer, top_transfer, coupling_tiles, send_index, leaf_list, top_list):
    f32 = jnp.float32
    bf16 = jnp.bfloat16
    ltop = N_LEAF.bit_length() - 1
    points = rhs_block.reshape(R, LEAVES, M).astype(f32)
    basis = leaf_basis.reshape(LEAVES, M, RANK).astype(f32)
    xleaf = jnp.einsum("blm,lmq->lbq", points, basis).astype(bf16)
    panels = xleaf.reshape(N_LEAF, LD, R, RANK)
    count = LD
    while count > 1:
        trans = local_transfer[:, count - 2:2 * count - 2].astype(f32)
        prods = jnp.einsum("nhbr,nhrq->nhbq", panels.astype(f32), trans)
        panels = prods.reshape(N_LEAF, count // 2, 2, R, RANK).sum(axis=2).astype(bf16)
        count = count // 2
    xtop = jnp.zeros((2 * N_LEAF, R, RANK), bf16)
    xtop = xtop.at[N_LEAF:].set(panels[:, 0])
    for level in range(ltop - 1, 1, -1):
        lo = 2 ** (level + 1)
        child = xtop[lo:2 * lo].astype(f32)
        trans = top_transfer[lo - 8:2 * lo - 8].astype(f32)
        prods = jnp.einsum("cbr,crq->cbq", child, trans)
        parent = prods.reshape(lo // 2, 2, R, RANK).sum(axis=1).astype(bf16)
        xtop = xtop.at[lo // 2:lo].set(parent)
    tgt = top_list[0]
    src = top_list[1]
    til = top_list[2]
    contrib = jnp.einsum("ebr,erq->ebq", xtop[src].astype(f32), coupling_tiles[til].astype(f32))
    ytop = jnp.zeros((2 * N_LEAF, R, RANK), f32).at[tgt].add(contrib)
    for level in range(3, ltop + 1):
        lo = 2 ** level
        parent = jnp.repeat(ytop[lo // 2:lo].astype(bf16), 2, axis=0).astype(f32)
        trans = top_transfer[lo - 8:2 * lo - 8].astype(f32)
        ytop = ytop.at[lo:2 * lo].add(jnp.einsum("cbq,crq->cbr", parent, trans))
    ydown = ytop[N_LEAF:][:, None]
    for level in range(1, LOG_LD + 1):
        lo = 2 ** level
        parent = jnp.repeat(ydown.astype(bf16), 2, axis=1).astype(f32)
        trans = local_transfer[:, lo - 2:2 * lo - 2].astype(f32)
        ydown = jnp.einsum("nhbq,nhrq->nhbr", parent, trans)
    ydown = ydown.reshape(LEAVES, R, RANK)
    slots = leaf_list[0]
    owner = (jnp.arange(LEAVES, dtype=jnp.int32) // LD)[:, None]
    sender = slots // C
    place = slots % C
    source = sender * LD + send_index[sender, owner, place]

    def couple(args):
        index, tile = args
        return jnp.einsum("ebr,erq->bq", xleaf[index].astype(f32), coupling_tiles[tile].astype(f32))

    coupled = lax.map(couple, (source, leaf_list[1]))
    wleaf = (ydown + coupled).astype(bf16)
    out = jnp.einsum("lbq,lmq->blm", wleaf.astype(f32), basis)
    return out.reshape(R, NPTS).astype(bf16)
```

```python
import functools

import jax
import jax.numpy as jnp
from jax import lax
from jax.experimental import pallas as pl
from jax.experimental.pallas import tpu as pltpu
from jax.sharding import PartitionSpec as P

F32 = jnp.float32
BF16 = jnp.bfloat16
MESH = pl.DeviceIdType.MESH
GROUP = 4
BROWS = 16


def dot(a, b):
    return jnp.dot(a, b, preferred_element_type=F32)


def dot_nt(a, b):
    return lax.dot_general(a, b, (((1,), (1,)), ((), ())), preferred_element_type=F32)


def kernel(
    nleaf,
    tlist_hbm,
    llist_hbm,
    send_hbm,
    rhs_hbm,
    basis_hbm,
    local_hbm,
    top_hbm,
    tiles_hbm,
    out_ref,
    rhs,
    basis,
    local,
    top,
    table,
    xleaf,
    send,
    recv,
    xtop,
    xroot,
    tally_f,
    tally,
    pool,
    summed,
    acc,
    picks,
    down,
    top_list,
    leaf_list,
    in_sem,
    own_sem,
    part_send,
    part_recv,
    far_send,
    far_recv,
    side_send,
    side_recv,
    fwd_send,
    fwd_recv,
    pan_send,
    pan_recv,
    root_send,
    root_recv,
):
    me = lax.axis_index("leaf")
    mr = lax.axis_index("rhs")
    leaves, entries = leaf_list.shape[1:]
    slots = picks.shape[0]
    width = rhs.shape[0]
    rank = basis.shape[1]
    points = basis.shape[0] // leaves
    ntl = tiles_hbm.shape[0]
    ntiles = table.shape[0]
    chunks = ntl // GROUP
    pool_rows = nleaf * slots
    ltop = nleaf.bit_length() - 1
    parts = width // BROWS

    barrier = pltpu.get_barrier_semaphore()
    for i in (1, 2):
        pl.semaphore_signal(barrier, inc=1, device_id={"rhs": mr ^ i}, device_id_type=MESH)
    for i in range(1, nleaf):
        pl.semaphore_signal(barrier, inc=1, device_id={"leaf": me ^ i}, device_id_type=MESH)

    loads = [
        pltpu.make_async_copy(src, dst, in_sem.at[i])
        for i, (src, dst) in enumerate(
            (
                (rhs_hbm, rhs),
                (basis_hbm, basis),
                (local_hbm.at[0], local),
                (top_hbm, top),
                (send_hbm.at[me], picks),
                (llist_hbm, leaf_list),
                (tlist_hbm, top_list),
            )
        )
    ]
    for i in (4, 0, 1, 2, 5, 6, 3):
        loads[i].start()
    own = pltpu.make_async_copy(tiles_hbm, table.at[pl.ds(mr * ntl, ntl)], own_sem)
    own.start()

    side = lax.rem(me, 2)
    last = chunks - 1

    def order(j):
        return (j + side * (last - 2 * j)) * GROUP

    def far_copy(j):
        return pltpu.make_async_remote_copy(
            src_ref=tiles_hbm.at[pl.ds(order(j), GROUP)],
            dst_ref=table.at[pl.ds(mr * ntl + order(j), GROUP)],
            send_sem=far_send.at[j],
            recv_sem=far_recv.at[j],
            device_id={"rhs": mr ^ 2},
            device_id_type=MESH,
        )

    def fwd_copy(j):
        rows = table.at[pl.ds((mr ^ 2) * ntl + order(j), GROUP)]
        return pltpu.make_async_remote_copy(
            src_ref=rows,
            dst_ref=rows,
            send_sem=fwd_send.at[j],
            recv_sem=fwd_recv.at[j],
            device_id={"rhs": mr ^ 1},
            device_id_type=MESH,
        )

    far = [far_copy(j) for j in range(last)]
    fwd = [fwd_copy(j) for j in range(chunks)]
    first = table.at[pl.ds((mr ^ 2) * ntl + order(0), GROUP)]
    across = pltpu.make_async_remote_copy(
        src_ref=first,
        dst_ref=first,
        send_sem=side_send,
        recv_sem=side_recv,
        device_id={"leaf": me ^ 1},
        device_id_type=MESH,
    )
    part = pltpu.make_async_remote_copy(
        src_ref=tiles_hbm,
        dst_ref=table.at[pl.ds(mr * ntl, ntl)],
        send_sem=part_send,
        recv_sem=part_recv,
        device_id={"rhs": mr ^ 1},
        device_id_type=MESH,
    )
    pl.semaphore_wait(barrier, nleaf + 1)
    for copy in far:
        copy.start()
    part.start()

    loads[4].wait()
    loads[0].wait()
    loads[1].wait()
    for g in range(leaves):
        cols = pl.ds(g * points, points)
        xleaf[g] = dot(rhs[:, cols], basis[cols, :]).astype(BF16)

    for i in range(1, nleaf):
        for c in range(slots):
            pick = jnp.maximum(picks[c, me ^ i], 0)
            send[i, :, c] = xleaf[pick].reshape(parts, BROWS, rank)

    panels = [
        [
            pltpu.make_async_remote_copy(
                src_ref=send.at[i, q],
                dst_ref=recv.at[i, q],
                send_sem=pan_send.at[i, q],
                recv_sem=pan_recv.at[i, q],
                device_id={"leaf": me ^ i},
                device_id_type=MESH,
            )
            for i in range(1, nleaf)
        ]
        for q in range(parts)
    ]
    for copy in panels[0][::-1]:
        copy.start()

    loads[2].wait()
    level = [xleaf[g] for g in range(leaves)]
    count = leaves
    while count > 1:
        level = [
            (
                dot(level[2 * h], local[count - 2 + 2 * h])
                + dot(level[2 * h + 1], local[count - 1 + 2 * h])
            ).astype(BF16)
            for h in range(count // 2)
        ]
        count //= 2
    xroot[...] = level[0]
    roots = []
    for i in range(2, nleaf - 1):
        copy = pltpu.make_async_remote_copy(
            src_ref=xroot,
            dst_ref=xtop.at[nleaf + me],
            send_sem=root_send.at[i],
            recv_sem=root_recv.at[i],
            device_id={"leaf": lax.rem(me + i, nleaf)},
            device_id_type=MESH,
        )
        copy.start()
        roots.append(copy)
    for q in range(1, parts):
        for copy in panels[q][::-1]:
            copy.start()
    for n in range(4):
        xtop[n] = jnp.zeros((width, rank), BF16)
    for i in (0, 1, nleaf - 1):
        xtop[nleaf + lax.rem(me + i, nleaf)] = jnp.zeros((width, rank), BF16)

    loads[5].wait()
    tile_ids = lax.broadcasted_iota(jnp.int32, (ntiles, entries), 0)
    slot_ids = lax.broadcasted_iota(jnp.int32, (pool_rows, entries), 0)
    for g in range(leaves):
        here = leaf_list[0, g : g + 1, :] ^ (me * slots)
        tile = leaf_list[1, g : g + 1, :]
        tile_hot = jnp.where(tile_ids == tile, 1.0, 0.0).astype(BF16)
        slot_hot = jnp.where(slot_ids == here, 1.0, 0.0).astype(BF16)
        tally_f[:, g, :] = dot_nt(tile_hot, slot_hot)
    tally[...] = tally_f[...].reshape(ntiles * leaves, pool_rows).astype(BF16)

    mats = []
    for h in range(2 * leaves - 2):
        step = local[h]
        mats.append(dot(step, mats[h // 2 - 1]).astype(BF16) if h >= 2 else step)
        if h >= leaves - 2:
            down[h - leaves + 2] = mats[h]

    for c in range(slots):
        pick = jnp.maximum(picks[c, me], 0)
        pool[:, c, :] = xleaf[pick].astype(F32)

    rows_per = 16 * leaves

    def tally_step(bp, carry):
        weights = jnp.concatenate([pool[2 * bp], pool[2 * bp + 1]], axis=1).astype(BF16)
        for m in range(ntiles // 16):
            res = dot(tally[m * rows_per : (m + 1) * rows_per, :], weights)
            res = res.astype(BF16).reshape(16 // GROUP, GROUP, leaves, 2 * rank)
            q = pl.ds(m * (16 // GROUP), 16 // GROUP)
            for k in range(GROUP):
                for b in range(2):
                    summed[q, 2 * bp + b, :, k * rank : (k + 1) * rank] = res[
                        :, k, :, b * rank : (b + 1) * rank
                    ]
        return carry

    def couple(groups, m):
        rows = pl.ds(m * BROWS, BROWS)
        total = None
        for q in groups:
            lhs = summed[q, rows].reshape(BROWS * leaves, GROUP * rank)
            res = dot(lhs, table[pl.ds(q * GROUP, GROUP)].reshape(GROUP * rank, rank))
            total = res if total is None else total + res
        return rows, total.reshape(BROWS, leaves, rank)

    def gather(q):
        for i in range(1, nleaf):
            panels[q][i - 1].wait_recv()
            for c in range(slots):
                pool[q * BROWS : (q + 1) * BROWS, i * slots + c, :] = recv[i, q, c].astype(F32)
        lax.fori_loop(q * BROWS // 2, (q + 1) * BROWS // 2, tally_step, 0, unroll=4)

    half = lax.div(mr, 2)
    near = [half * (2 * chunks) + c for c in range(2 * chunks)]
    away = [(1 - half) * (2 * chunks) + c for c in range(2 * chunks)]
    early = parts // 2
    for q in range(early):
        if q == 0:
            far[0].wait_recv()
            fwd[0].start()
            across.start()
        gather(q)
        if q == 0:
            own.wait()
            part.wait_recv()
        rows, total = couple(near, q)
        acc[rows] = total
        if q == 0:
            far[1].wait_recv()
            fwd[1].start()
    for j in range(2, last):
        far[j].wait_recv()
        fwd[j].start()
    across.wait_recv()
    fwd[last].start()

    for copy in roots:
        copy.wait_recv()
    loads[3].wait()
    loads[6].wait()
    for lev in range(ltop - 1, 1, -1):
        for n in range(2**lev, 2 ** (lev + 1)):
            both = dot(xtop[2 * n], top[2 * n - 8]) + dot(xtop[2 * n + 1], top[2 * n - 7])
            xtop[n] = both.astype(BF16)

    for copy in fwd:
        copy.wait_recv()
    for q in range(early):
        rows, total = couple(away, q)
        acc[rows] = acc[rows] + total

    node = nleaf + me
    depth = ltop - 1

    batch = 8

    def top_step(e, total):
        lhs = [[] for _ in range(depth)]
        rhs_mats = []
        for k in range(batch):
            at = e * batch + k
            target = top_list[0, at]
            x = xtop[top_list[1, at]].astype(F32)
            rhs_mats.append(table[top_list[2, at]])
            for j in range(depth):
                keep = jnp.where(target == lax.shift_right_logical(node, j), 1.0, 0.0)
                lhs[j].append((x * keep).astype(BF16))
        wide = jnp.concatenate([jnp.concatenate(row, axis=1) for row in lhs], axis=0)
        return total + dot(wide, jnp.concatenate(rhs_mats, axis=0))

    zero = jnp.zeros((depth * width, rank), F32)
    total = lax.fori_loop(0, top_list.shape[1] // batch, top_step, zero, unroll=2)
    ys = [total[j * width : (j + 1) * width] for j in range(depth)]
    y = ys[depth - 1]
    for j in range(depth - 2, -1, -1):
        y = ys[j] + dot_nt(y.astype(BF16), top[lax.shift_right_logical(node, j) - 8])

    y = y.astype(BF16)
    for q in range(early, parts):
        gather(q)
        rows, total = couple(near + away, q)
        acc[rows] = total
    for g in range(leaves):
        wleaf = (acc[:, g, :] + dot_nt(y, down[g])).astype(BF16)
        cols = pl.ds(g * points, points)
        out_ref[:, cols] = dot_nt(wleaf, basis[cols, :]).astype(BF16)

    part.wait_send()
    across.wait_send()
    for copy in far + fwd + sum(panels, []) + roots:
        copy.wait_send()


def shards(
    nleaf,
    nrhs,
    rhs_block,
    leaf_basis,
    local_transfer,
    top_transfer,
    coupling_tiles,
    send_index,
    leaf_list,
    top_list,
):
    leaves = leaf_list.shape[1]
    width, npts = rhs_block.shape
    rank = leaf_basis.shape[1]
    slots = send_index.shape[2]
    ntl = coupling_tiles.shape[0]
    ntiles = ntl * nrhs
    pool_rows = nleaf * slots
    chunks = ntl // GROUP
    vmem = pl.BlockSpec(memory_space=pltpu.VMEM)
    hbm = pl.BlockSpec(memory_space=pltpu.HBM)
    operands = (
        top_list,
        leaf_list,
        jnp.transpose(send_index, (0, 2, 1)),
        rhs_block,
        leaf_basis,
        local_transfer,
        top_transfer,
        coupling_tiles,
    )
    dma = pltpu.SemaphoreType.DMA
    room = 40 if nleaf <= 16 else 60
    return pl.pallas_call(
        functools.partial(kernel, nleaf),
        out_shape=jax.ShapeDtypeStruct((width, npts), BF16),
        in_specs=[hbm] * len(operands),
        out_specs=vmem,
        scratch_shapes=[
            pltpu.VMEM((width, npts), BF16),
            pltpu.VMEM(leaf_basis.shape, BF16),
            pltpu.VMEM(local_transfer.shape[1:], BF16),
            pltpu.VMEM(top_transfer.shape, BF16),
            pltpu.VMEM((ntiles, rank, rank), BF16),
            pltpu.VMEM((leaves, width, rank), BF16),
            pltpu.VMEM((nleaf, width // BROWS, slots, BROWS, rank), BF16),
            pltpu.VMEM((nleaf, width // BROWS, slots, BROWS, rank), BF16),
            pltpu.VMEM((2 * nleaf, width, rank), BF16),
            pltpu.VMEM((width, rank), BF16),
            pltpu.VMEM((ntiles, leaves, pool_rows), F32),
            pltpu.VMEM((ntiles * leaves, pool_rows), BF16),
            pltpu.VMEM((width, pool_rows, rank), F32),
            pltpu.VMEM((ntiles // GROUP, width, leaves, GROUP * rank), BF16),
            pltpu.VMEM((width, leaves, rank), F32),
            pltpu.SMEM((slots, nleaf), jnp.int32),
            pltpu.VMEM((leaves, rank, rank), BF16),
            pltpu.SMEM(top_list.shape, jnp.int32),
            pltpu.VMEM(leaf_list.shape, jnp.int32),
            dma((7,)),
            dma,
            dma,
            dma,
            dma((chunks,)),
            dma((chunks,)),
            dma,
            dma,
            dma((chunks,)),
            dma((chunks,)),
            dma((nleaf, width // BROWS)),
            dma((nleaf, width // BROWS)),
            dma((nleaf,)),
            dma((nleaf,)),
        ],
        compiler_params=pltpu.CompilerParams(
            collective_id=0, has_side_effects=True, vmem_limit_bytes=room * 1024 * 1024
        ),
        name="far_field",
    )(*(pltpu.with_memory_space_constraint(a, pltpu.HBM) for a in operands))


def solution(mesh):
    placed = (
        P("rhs", "leaf"),
        P("leaf", None),
        P("leaf", None, None, None),
        P(),
        P("rhs", None, None),
        P(),
        P(None, "leaf", None),
        P(),
    )
    body = functools.partial(shards, mesh.shape["leaf"], mesh.shape["rhs"])
    return jax.shard_map(
        body, mesh=mesh, in_specs=placed, out_specs=P("rhs", "leaf"), check_vma=False
    )
```

```python
import functools

import jax
import jax.numpy as jnp
from jax import lax
from jax.experimental import pallas as pl
from jax.experimental.pallas import tpu as pltpu
from jax.sharding import PartitionSpec as P

F32 = jnp.float32
BF16 = jnp.bfloat16
MESH = pl.DeviceIdType.MESH
GROUP = 4
CHUNK = 2
CUTS = (0, 1, 3, 5, 7, 8)


def dot(a, b):
    return jnp.dot(a, b, preferred_element_type=F32)


def dot_nt(a, b):
    return lax.dot_general(a, b, (((1,), (1,)), ((), ())), preferred_element_type=F32)


def kernel(
    nleaf,
    tlist_hbm,
    llist_hbm,
    send_hbm,
    rhs_hbm,
    basis_hbm,
    local_hbm,
    top_hbm,
    tiles_hbm,
    out_ref,
    rhs,
    basis,
    local,
    top,
    table,
    xleaf,
    send,
    recv,
    xtop,
    xroot,
    tally_f,
    tally,
    pool,
    summed,
    acc,
    picks,
    down,
    top_list,
    leaf_list,
    in_sem,
    own_sem,
    part_send,
    part_recv,
    far_send,
    far_recv,
    side_send,
    side_recv,
    fwd_send,
    fwd_recv,
    pan_send,
    pan_recv,
    root_send,
    root_recv,
):
    me = lax.axis_index("leaf")
    mr = lax.axis_index("rhs")
    leaves, entries = leaf_list.shape[1:]
    slots = picks.shape[0]
    width = rhs.shape[0]
    rank = basis.shape[1]
    points = basis.shape[0] // leaves
    ntl = tiles_hbm.shape[0]
    ntiles = table.shape[0]
    groups = ntl // GROUP
    chunks = ntl // CHUNK
    pool_rows = nleaf * slots
    ltop = nleaf.bit_length() - 1
    cuts = [width * c // 8 for c in CUTS]
    parts = len(cuts) - 1

    barrier = pltpu.get_barrier_semaphore()
    for i in (1, 2):
        pl.semaphore_signal(barrier, inc=1, device_id={"rhs": mr ^ i}, device_id_type=MESH)
    for i in range(1, nleaf):
        pl.semaphore_signal(barrier, inc=1, device_id={"leaf": me ^ i}, device_id_type=MESH)

    loads = [
        pltpu.make_async_copy(src, dst, in_sem.at[i])
        for i, (src, dst) in enumerate(
            (
                (rhs_hbm, rhs),
                (basis_hbm, basis),
                (local_hbm.at[0], local),
                (top_hbm, top),
                (send_hbm.at[me], picks),
                (llist_hbm, leaf_list),
                (tlist_hbm, top_list),
            )
        )
    ]
    for i in (4, 0, 1, 2, 5, 6, 3):
        loads[i].start()
    own = pltpu.make_async_copy(tiles_hbm, table.at[pl.ds(mr * ntl, ntl)], own_sem)
    own.start()

    side = lax.rem(me, 2)
    borrowed = (chunks - 1) // 2
    direct = chunks - borrowed

    def rows_of(j, flip):
        at = (j + (side ^ flip) * (chunks - 1 - 2 * j)) * CHUNK
        return at, table.at[pl.ds((mr ^ 2) * ntl + at, CHUNK)]

    def far_copy(j):
        at, _ = rows_of(j, 0)
        return pltpu.make_async_remote_copy(
            src_ref=tiles_hbm.at[pl.ds(at, CHUNK)],
            dst_ref=table.at[pl.ds(mr * ntl + at, CHUNK)],
            send_sem=far_send.at[j],
            recv_sem=far_recv.at[j],
            device_id={"rhs": mr ^ 2},
            device_id_type=MESH,
        )

    def side_copy(j):
        _, rows = rows_of(j, 0)
        return pltpu.make_async_remote_copy(
            src_ref=rows,
            dst_ref=rows,
            send_sem=side_send.at[j],
            recv_sem=side_recv.at[j],
            device_id={"leaf": me ^ 1},
            device_id_type=MESH,
        )

    def fwd_copy(k):
        _, rows = rows_of(k, 0) if k < direct else rows_of(k - direct, 1)
        return pltpu.make_async_remote_copy(
            src_ref=rows,
            dst_ref=rows,
            send_sem=fwd_send.at[k],
            recv_sem=fwd_recv.at[k],
            device_id={"rhs": mr ^ 1},
            device_id_type=MESH,
        )

    far = [far_copy(j) for j in range(direct)]
    across = [side_copy(j) for j in range(borrowed)]
    fwd = [fwd_copy(k) for k in range(chunks)]

    def pass_far(j):
        far[j].wait_recv()
        fwd[j].start()
        if j < borrowed:
            across[j].start()

    def pass_across(j):
        across[j].wait_recv()
        fwd[direct + j].start()

    part = pltpu.make_async_remote_copy(
        src_ref=tiles_hbm,
        dst_ref=table.at[pl.ds(mr * ntl, ntl)],
        send_sem=part_send,
        recv_sem=part_recv,
        device_id={"rhs": mr ^ 1},
        device_id_type=MESH,
    )
    pl.semaphore_wait(barrier, nleaf + 1)
    for copy in far:
        copy.start()
    part.start()

    loads[4].wait()
    loads[0].wait()
    loads[1].wait()
    for g in range(leaves):
        cols = pl.ds(g * points, points)
        xleaf[g] = dot(rhs[:, cols], basis[cols, :]).astype(BF16)

    for i in range(1, nleaf):
        for c in range(slots):
            pick = jnp.maximum(picks[c, me ^ i], 0)
            panel = xleaf[pick]
            for lo, hi in zip(cuts[:-1], cuts[1:]):
                at = lo * slots + c * (hi - lo)
                send[i, at : at + hi - lo] = panel[lo:hi]

    panels = [
        [
            pltpu.make_async_remote_copy(
                src_ref=send.at[i, pl.ds(cuts[q] * slots, (cuts[q + 1] - cuts[q]) * slots)],
                dst_ref=recv.at[i, pl.ds(cuts[q] * slots, (cuts[q + 1] - cuts[q]) * slots)],
                send_sem=pan_send.at[i, q],
                recv_sem=pan_recv.at[i, q],
                device_id={"leaf": me ^ i},
                device_id_type=MESH,
            )
            for i in range(1, nleaf)
        ]
        for q in range(parts)
    ]
    for copy in panels[0][::-1]:
        copy.start()

    loads[2].wait()
    level = [xleaf[g] for g in range(leaves)]
    count = leaves
    while count > 1:
        level = [
            (
                dot(level[2 * h], local[count - 2 + 2 * h])
                + dot(level[2 * h + 1], local[count - 1 + 2 * h])
            ).astype(BF16)
            for h in range(count // 2)
        ]
        count //= 2
    xroot[...] = level[0]
    roots = []
    for i in range(2, nleaf - 1):
        copy = pltpu.make_async_remote_copy(
            src_ref=xroot,
            dst_ref=xtop.at[nleaf + me],
            send_sem=root_send.at[i],
            recv_sem=root_recv.at[i],
            device_id={"leaf": lax.rem(me + i, nleaf)},
            device_id_type=MESH,
        )
        copy.start()
        roots.append(copy)
    for copy in panels[1][::-1]:
        copy.start()
    for n in range(4):
        xtop[n] = jnp.zeros((width, rank), BF16)
    for i in (0, 1, nleaf - 1):
        xtop[nleaf + lax.rem(me + i, nleaf)] = jnp.zeros((width, rank), BF16)

    loads[5].wait()
    tile_ids = lax.broadcasted_iota(jnp.int32, (ntiles, entries), 0)
    slot_ids = lax.broadcasted_iota(jnp.int32, (pool_rows, entries), 0)
    for g in range(leaves):
        here = leaf_list[0, g : g + 1, :] ^ (me * slots)
        tile = leaf_list[1, g : g + 1, :]
        tile_hot = jnp.where(tile_ids == tile, 1.0, 0.0).astype(BF16)
        slot_hot = jnp.where(slot_ids == here, 1.0, 0.0).astype(BF16)
        tally_f[:, g, :] = dot_nt(tile_hot, slot_hot)
    tally[...] = tally_f[...].reshape(ntiles * leaves, pool_rows).astype(BF16)

    mats = []
    for h in range(2 * leaves - 2):
        step = local[h]
        mats.append(dot(step, mats[h // 2 - 1]).astype(BF16) if h >= 2 else step)
        if h >= leaves - 2:
            down[h - leaves + 2] = mats[h]

    for c in range(slots):
        pick = jnp.maximum(picks[c, me], 0)
        pool[:, c, :] = xleaf[pick].astype(F32)

    rows_per = 16 * leaves

    def tally_step(bp, carry):
        weights = jnp.concatenate([pool[2 * bp], pool[2 * bp + 1]], axis=1).astype(BF16)
        for m in range(ntiles // 16):
            res = dot(tally[m * rows_per : (m + 1) * rows_per, :], weights)
            res = res.astype(BF16).reshape(16 // GROUP, GROUP, leaves, 2 * rank)
            q = pl.ds(m * (16 // GROUP), 16 // GROUP)
            for k in range(GROUP):
                for b in range(2):
                    summed[q, 2 * bp + b, :, k * rank : (k + 1) * rank] = res[
                        :, k, :, b * rank : (b + 1) * rank
                    ]
        return carry

    def couple(picked, q):
        lo, hi = cuts[q], cuts[q + 1]
        total = None
        for k in picked:
            lhs = summed[k, lo:hi].reshape((hi - lo) * leaves, GROUP * rank)
            res = dot(lhs, table[pl.ds(k * GROUP, GROUP)].reshape(GROUP * rank, rank))
            total = res if total is None else total + res
        return total.reshape(hi - lo, leaves, rank)

    def gather(q):
        lo, hi = cuts[q], cuts[q + 1]
        for copy in panels[q]:
            copy.wait_send()
        if q + 2 < parts:
            for copy in panels[q + 2][::-1]:
                copy.start()
        for i in range(1, nleaf):
            panels[q][i - 1].wait_recv()
            for c in range(slots):
                at = lo * slots + c * (hi - lo)
                pool[lo:hi, i * slots + c, :] = recv[i, at : at + hi - lo].astype(F32)
        lax.fori_loop(lo // 2, hi // 2, tally_step, 0, unroll=4)

    half = lax.div(mr, 2)
    near = [half * (2 * groups) + c for c in range(2 * groups)]
    away = [(1 - half) * (2 * groups) + c for c in range(2 * groups)]
    for j in range(borrowed):
        pass_far(j)
    own.wait()
    part.wait_recv()
    early = 2
    for q in range(early):
        gather(q)
        acc[cuts[q] : cuts[q + 1]] = couple(near, q)
        if q == 0:
            for j in range(borrowed, direct):
                pass_far(j)
    for j in range(borrowed):
        pass_across(j)

    for copy in roots:
        copy.wait_recv()
    loads[3].wait()
    loads[6].wait()
    for lev in range(ltop - 1, 1, -1):
        for n in range(2**lev, 2 ** (lev + 1)):
            both = dot(xtop[2 * n], top[2 * n - 8]) + dot(xtop[2 * n + 1], top[2 * n - 7])
            xtop[n] = both.astype(BF16)

    gather(early)
    for copy in fwd:
        copy.wait_recv()
    for q in range(early):
        acc[cuts[q] : cuts[q + 1]] = acc[cuts[q] : cuts[q + 1]] + couple(away, q)
    acc[cuts[early] : cuts[early + 1]] = couple(near + away, early)

    node = nleaf + me
    depth = ltop - 1

    batch = 8

    def top_step(e, total):
        lhs = [[] for _ in range(depth)]
        rhs_mats = []
        for k in range(batch):
            at = e * batch + k
            target = top_list[0, at]
            x = xtop[top_list[1, at]].astype(F32)
            rhs_mats.append(table[top_list[2, at]])
            for j in range(depth):
                keep = jnp.where(target == lax.shift_right_logical(node, j), 1.0, 0.0)
                lhs[j].append((x * keep).astype(BF16))
        wide = jnp.concatenate([jnp.concatenate(row, axis=1) for row in lhs], axis=0)
        return total + dot(wide, jnp.concatenate(rhs_mats, axis=0))

    zero = jnp.zeros((depth * width, rank), F32)
    total = lax.fori_loop(0, top_list.shape[1] // batch, top_step, zero, unroll=4)
    ys = [total[j * width : (j + 1) * width] for j in range(depth)]
    y = ys[depth - 1]
    for j in range(depth - 2, -1, -1):
        y = ys[j] + dot_nt(y.astype(BF16), top[lax.shift_right_logical(node, j) - 8])

    y = y.astype(BF16)
    for q in range(early + 1, parts):
        gather(q)
        acc[cuts[q] : cuts[q + 1]] = couple(near + away, q)
    for g in range(leaves):
        wleaf = (acc[:, g, :] + dot_nt(y, down[g])).astype(BF16)
        cols = pl.ds(g * points, points)
        out_ref[:, cols] = dot_nt(wleaf, basis[cols, :]).astype(BF16)

    part.wait_send()
    for copy in far + across + fwd + roots:
        copy.wait_send()


def shards(
    nleaf,
    nrhs,
    rhs_block,
    leaf_basis,
    local_transfer,
    top_transfer,
    coupling_tiles,
    send_index,
    leaf_list,
    top_list,
):
    leaves = leaf_list.shape[1]
    width, npts = rhs_block.shape
    rank = leaf_basis.shape[1]
    slots = send_index.shape[2]
    ntl = coupling_tiles.shape[0]
    ntiles = ntl * nrhs
    pool_rows = nleaf * slots
    chunks = ntl // CHUNK
    vmem = pl.BlockSpec(memory_space=pltpu.VMEM)
    hbm = pl.BlockSpec(memory_space=pltpu.HBM)
    operands = (
        top_list,
        leaf_list,
        jnp.transpose(send_index, (0, 2, 1)),
        rhs_block,
        leaf_basis,
        local_transfer,
        top_transfer,
        coupling_tiles,
    )
    dma = pltpu.SemaphoreType.DMA
    room = 40 if nleaf <= 16 else 60
    return pl.pallas_call(
        functools.partial(kernel, nleaf),
        out_shape=jax.ShapeDtypeStruct((width, npts), BF16),
        in_specs=[hbm] * len(operands),
        out_specs=vmem,
        scratch_shapes=[
            pltpu.VMEM((width, npts), BF16),
            pltpu.VMEM(leaf_basis.shape, BF16),
            pltpu.VMEM(local_transfer.shape[1:], BF16),
            pltpu.VMEM(top_transfer.shape, BF16),
            pltpu.VMEM((ntiles, rank, rank), BF16),
            pltpu.VMEM((leaves, width, rank), BF16),
            pltpu.VMEM((nleaf, slots * width, rank), BF16),
            pltpu.VMEM((nleaf, slots * width, rank), BF16),
            pltpu.VMEM((2 * nleaf, width, rank), BF16),
            pltpu.VMEM((width, rank), BF16),
            pltpu.VMEM((ntiles, leaves, pool_rows), F32),
            pltpu.VMEM((ntiles * leaves, pool_rows), BF16),
            pltpu.VMEM((width, pool_rows, rank), F32),
            pltpu.VMEM((ntiles // GROUP, width, leaves, GROUP * rank), BF16),
            pltpu.VMEM((width, leaves, rank), F32),
            pltpu.SMEM((slots, nleaf), jnp.int32),
            pltpu.VMEM((leaves, rank, rank), BF16),
            pltpu.SMEM(top_list.shape, jnp.int32),
            pltpu.VMEM(leaf_list.shape, jnp.int32),
            dma((7,)),
            dma,
            dma,
            dma,
            dma((chunks,)),
            dma((chunks,)),
            dma((chunks,)),
            dma((chunks,)),
            dma((chunks,)),
            dma((chunks,)),
            dma((nleaf, len(CUTS) - 1)),
            dma((nleaf, len(CUTS) - 1)),
            dma((nleaf,)),
            dma((nleaf,)),
        ],
        compiler_params=pltpu.CompilerParams(
            collective_id=0, has_side_effects=True, vmem_limit_bytes=room * 1024 * 1024
        ),
        name="far_field",
    )(*(pltpu.with_memory_space_constraint(a, pltpu.HBM) for a in operands))


def solution(mesh):
    placed = (
        P("rhs", "leaf"),
        P("leaf", None),
        P("leaf", None, None, None),
        P(),
        P("rhs", None, None),
        P(),
        P(None, "leaf", None),
        P(),
    )
    body = functools.partial(shards, mesh.shape["leaf"], mesh.shape["rhs"])
    return jax.shard_map(
        body, mesh=mesh, in_specs=placed, out_specs=P("rhs", "leaf"), check_vma=False
    )
```

```python
import functools

import jax
import jax.numpy as jnp
from jax import lax
from jax.experimental import pallas as pl
from jax.experimental.pallas import tpu as pltpu
from jax.sharding import PartitionSpec as P

F32 = jnp.float32
BF16 = jnp.bfloat16
MESH = pl.DeviceIdType.MESH
GROUP = 4
CHUNK = 2
CUTS = (0, 1, 3, 5, 7, 8)


def dot(a, b):
    return jnp.dot(a, b, preferred_element_type=F32)


def dot_nt(a, b):
    return lax.dot_general(a, b, (((1,), (1,)), ((), ())), preferred_element_type=F32)


def kernel(
    nleaf,
    tlist_hbm,
    llist_hbm,
    send_hbm,
    rhs_hbm,
    basis_hbm,
    local_hbm,
    top_hbm,
    tiles_hbm,
    out_ref,
    rhs,
    basis,
    local,
    top,
    table,
    xleaf,
    send,
    recv,
    xtop,
    xroot,
    tally_f,
    tally,
    pool,
    summed,
    acc,
    picks,
    down,
    top_list,
    leaf_list,
    in_sem,
    own_sem,
    part_send,
    part_recv,
    far_send,
    far_recv,
    side_send,
    side_recv,
    fwd_send,
    fwd_recv,
    pan_send,
    pan_recv,
    root_send,
    root_recv,
):
    me = lax.axis_index("leaf")
    mr = lax.axis_index("rhs")
    leaves, entries = leaf_list.shape[1:]
    slots = picks.shape[0]
    width = rhs.shape[0]
    rank = basis.shape[1]
    points = basis.shape[0] // leaves
    ntl = tiles_hbm.shape[0]
    ntiles = table.shape[0]
    groups = ntl // GROUP
    chunks = ntl // CHUNK
    pool_rows = nleaf * slots
    ltop = nleaf.bit_length() - 1
    cuts = [width * c // 8 for c in CUTS]
    parts = len(cuts) - 1

    barrier = pltpu.get_barrier_semaphore()
    for i in (1, 2):
        pl.semaphore_signal(barrier, inc=1, device_id={"rhs": mr ^ i}, device_id_type=MESH)
    for i in range(1, nleaf):
        pl.semaphore_signal(barrier, inc=1, device_id={"leaf": me ^ i}, device_id_type=MESH)

    loads = [
        pltpu.make_async_copy(src, dst, in_sem.at[i])
        for i, (src, dst) in enumerate(
            (
                (rhs_hbm, rhs),
                (basis_hbm, basis),
                (local_hbm.at[0], local),
                (top_hbm, top),
                (send_hbm.at[me], picks),
                (llist_hbm, leaf_list),
                (tlist_hbm, top_list),
            )
        )
    ]
    for i in (4, 0, 1, 2, 5, 6, 3):
        loads[i].start()
    own = pltpu.make_async_copy(tiles_hbm, table.at[pl.ds(mr * ntl, ntl)], own_sem)
    own.start()

    side = lax.rem(me, 2)
    borrowed = (chunks - 1) // 2
    direct = chunks - borrowed

    def rows_of(j, flip):
        at = (j + (side ^ flip) * (chunks - 1 - 2 * j)) * CHUNK
        return at, table.at[pl.ds((mr ^ 2) * ntl + at, CHUNK)]

    def far_copy(j):
        at, _ = rows_of(j, 0)
        return pltpu.make_async_remote_copy(
            src_ref=tiles_hbm.at[pl.ds(at, CHUNK)],
            dst_ref=table.at[pl.ds(mr * ntl + at, CHUNK)],
            send_sem=far_send.at[j],
            recv_sem=far_recv.at[j],
            device_id={"rhs": mr ^ 2},
            device_id_type=MESH,
        )

    def side_copy(j):
        _, rows = rows_of(j, 0)
        return pltpu.make_async_remote_copy(
            src_ref=rows,
            dst_ref=rows,
            send_sem=side_send.at[j],
            recv_sem=side_recv.at[j],
            device_id={"leaf": me ^ 1},
            device_id_type=MESH,
        )

    def fwd_copy(k):
        _, rows = rows_of(k, 0) if k < direct else rows_of(k - direct, 1)
        return pltpu.make_async_remote_copy(
            src_ref=rows,
            dst_ref=rows,
            send_sem=fwd_send.at[k],
            recv_sem=fwd_recv.at[k],
            device_id={"rhs": mr ^ 1},
            device_id_type=MESH,
        )

    far = [far_copy(j) for j in range(direct)]
    across = [side_copy(j) for j in range(borrowed)]
    fwd = [fwd_copy(k) for k in range(chunks)]

    def pass_far(j):
        far[j].wait_recv()
        fwd[j].start()
        if j < borrowed:
            across[j].start()

    def pass_across(j):
        across[j].wait_recv()
        fwd[direct + j].start()

    part = pltpu.make_async_remote_copy(
        src_ref=tiles_hbm,
        dst_ref=table.at[pl.ds(mr * ntl, ntl)],
        send_sem=part_send,
        recv_sem=part_recv,
        device_id={"rhs": mr ^ 1},
        device_id_type=MESH,
    )
    pl.semaphore_wait(barrier, nleaf + 1)
    for copy in far:
        copy.start()
    part.start()

    loads[4].wait()
    loads[0].wait()
    loads[1].wait()
    for g in range(leaves):
        cols = pl.ds(g * points, points)
        xleaf[g] = dot(rhs[:, cols], basis[cols, :]).astype(BF16)

    for i in range(1, nleaf):
        for c in range(slots):
            pick = jnp.maximum(picks[c, me ^ i], 0)
            panel = xleaf[pick]
            for lo, hi in zip(cuts[:-1], cuts[1:]):
                at = lo * slots + c * (hi - lo)
                send[i, at : at + hi - lo] = panel[lo:hi]

    panels = [
        [
            pltpu.make_async_remote_copy(
                src_ref=send.at[i, pl.ds(cuts[q] * slots, (cuts[q + 1] - cuts[q]) * slots)],
                dst_ref=recv.at[i, pl.ds(cuts[q] * slots, (cuts[q + 1] - cuts[q]) * slots)],
                send_sem=pan_send.at[i, q],
                recv_sem=pan_recv.at[i, q],
                device_id={"leaf": me ^ i},
                device_id_type=MESH,
            )
            for i in range(1, nleaf)
        ]
        for q in range(parts)
    ]
    for copy in panels[0]:
        copy.start()

    loads[2].wait()
    level = [xleaf[g] for g in range(leaves)]
    count = leaves
    while count > 1:
        level = [
            (
                dot(level[2 * h], local[count - 2 + 2 * h])
                + dot(level[2 * h + 1], local[count - 1 + 2 * h])
            ).astype(BF16)
            for h in range(count // 2)
        ]
        count //= 2
    xroot[...] = level[0]
    roots = []
    for i in range(2, nleaf - 1):
        copy = pltpu.make_async_remote_copy(
            src_ref=xroot,
            dst_ref=xtop.at[nleaf + me],
            send_sem=root_send.at[i],
            recv_sem=root_recv.at[i],
            device_id={"leaf": lax.rem(me + i, nleaf)},
            device_id_type=MESH,
        )
        copy.start()
        roots.append(copy)
    for copy in panels[1]:
        copy.start()
    for n in range(4):
        xtop[n] = jnp.zeros((width, rank), BF16)
    for i in (0, 1, nleaf - 1):
        xtop[nleaf + lax.rem(me + i, nleaf)] = jnp.zeros((width, rank), BF16)

    loads[5].wait()
    tile_ids = lax.broadcasted_iota(jnp.int32, (ntiles, entries), 0)
    slot_ids = lax.broadcasted_iota(jnp.int32, (pool_rows, entries), 0)
    for g in range(leaves):
        here = leaf_list[0, g : g + 1, :] ^ (me * slots)
        tile = leaf_list[1, g : g + 1, :]
        tile_hot = jnp.where(tile_ids == tile, 1.0, 0.0).astype(BF16)
        slot_hot = jnp.where(slot_ids == here, 1.0, 0.0).astype(BF16)
        tally_f[:, g, :] = dot_nt(tile_hot, slot_hot)
    tally[...] = tally_f[...].reshape(ntiles * leaves, pool_rows).astype(BF16)

    mats = []
    for h in range(2 * leaves - 2):
        step = local[h]
        mats.append(dot(step, mats[h // 2 - 1]).astype(BF16) if h >= 2 else step)
        if h >= leaves - 2:
            down[h - leaves + 2] = mats[h]

    for c in range(slots):
        pick = jnp.maximum(picks[c, me], 0)
        pool[:, c, :] = xleaf[pick].astype(F32)

    rows_per = 16 * leaves

    def tally_step(bp, carry):
        weights = jnp.concatenate([pool[2 * bp], pool[2 * bp + 1]], axis=1).astype(BF16)
        for m in range(ntiles // 16):
            res = dot(tally[m * rows_per : (m + 1) * rows_per, :], weights)
            res = res.astype(BF16).reshape(16 // GROUP, GROUP, leaves, 2 * rank)
            q = pl.ds(m * (16 // GROUP), 16 // GROUP)
            for k in range(GROUP):
                for b in range(2):
                    summed[q, 2 * bp + b, :, k * rank : (k + 1) * rank] = res[
                        :, k, :, b * rank : (b + 1) * rank
                    ]
        return carry

    def couple(picked, q):
        lo, hi = cuts[q], cuts[q + 1]
        total = None
        for k in picked:
            lhs = summed[k, lo:hi].reshape((hi - lo) * leaves, GROUP * rank)
            res = dot(lhs, table[pl.ds(k * GROUP, GROUP)].reshape(GROUP * rank, rank))
            total = res if total is None else total + res
        return total.reshape(hi - lo, leaves, rank)

    def gather(q):
        lo, hi = cuts[q], cuts[q + 1]
        for copy in panels[q]:
            copy.wait_send()
        if q + 2 < parts:
            for copy in panels[q + 2]:
                copy.start()
        for i in range(1, nleaf):
            panels[q][i - 1].wait_recv()
            for c in range(slots):
                at = lo * slots + c * (hi - lo)
                pool[lo:hi, i * slots + c, :] = recv[i, at : at + hi - lo].astype(F32)
        lax.fori_loop(lo // 2, hi // 2, tally_step, 0, unroll=4)

    half = lax.div(mr, 2)
    near = [half * (2 * groups) + c for c in range(2 * groups)]
    away = [(1 - half) * (2 * groups) + c for c in range(2 * groups)]
    for j in range(borrowed):
        pass_far(j)
    own.wait()
    part.wait_recv()
    early = 2
    for q in range(early):
        gather(q)
        acc[cuts[q] : cuts[q + 1]] = couple(near, q)
        if q == 0:
            for j in range(borrowed, direct):
                pass_far(j)
    for j in range(borrowed):
        pass_across(j)

    for copy in roots:
        copy.wait_recv()
    loads[3].wait()
    loads[6].wait()
    for lev in range(ltop - 1, 1, -1):
        for n in range(2**lev, 2 ** (lev + 1)):
            both = dot(xtop[2 * n], top[2 * n - 8]) + dot(xtop[2 * n + 1], top[2 * n - 7])
            xtop[n] = both.astype(BF16)

    gather(early)
    for copy in fwd:
        copy.wait_recv()
    for q in range(early):
        acc[cuts[q] : cuts[q + 1]] = acc[cuts[q] : cuts[q + 1]] + couple(away, q)
    acc[cuts[early] : cuts[early + 1]] = couple(near + away, early)

    node = nleaf + me
    depth = ltop - 1

    batch = 8

    def top_step(e, total):
        lhs = [[] for _ in range(depth)]
        rhs_mats = []
        for k in range(batch):
            at = e * batch + k
            target = top_list[0, at]
            x = xtop[top_list[1, at]].astype(F32)
            rhs_mats.append(table[top_list[2, at]])
            for j in range(depth):
                keep = jnp.where(target == lax.shift_right_logical(node, j), 1.0, 0.0)
                lhs[j].append((x * keep).astype(BF16))
        wide = jnp.concatenate([jnp.concatenate(row, axis=1) for row in lhs], axis=0)
        return total + dot(wide, jnp.concatenate(rhs_mats, axis=0))

    zero = jnp.zeros((depth * width, rank), F32)
    total = lax.fori_loop(0, top_list.shape[1] // batch, top_step, zero, unroll=4)
    ys = [total[j * width : (j + 1) * width] for j in range(depth)]
    y = ys[depth - 1]
    for j in range(depth - 2, -1, -1):
        y = ys[j] + dot_nt(y.astype(BF16), top[lax.shift_right_logical(node, j) - 8])

    y = y.astype(BF16)
    for q in range(early + 1, parts):
        gather(q)
        acc[cuts[q] : cuts[q + 1]] = couple(near + away, q)
    for g in range(leaves):
        wleaf = (acc[:, g, :] + dot_nt(y, down[g])).astype(BF16)
        cols = pl.ds(g * points, points)
        out_ref[:, cols] = dot_nt(wleaf, basis[cols, :]).astype(BF16)

    part.wait_send()
    for copy in far + across + fwd + roots:
        copy.wait_send()


def shards(
    nleaf,
    nrhs,
    rhs_block,
    leaf_basis,
    local_transfer,
    top_transfer,
    coupling_tiles,
    send_index,
    leaf_list,
    top_list,
):
    leaves = leaf_list.shape[1]
    width, npts = rhs_block.shape
    rank = leaf_basis.shape[1]
    slots = send_index.shape[2]
    ntl = coupling_tiles.shape[0]
    ntiles = ntl * nrhs
    pool_rows = nleaf * slots
    chunks = ntl // CHUNK
    vmem = pl.BlockSpec(memory_space=pltpu.VMEM)
    hbm = pl.BlockSpec(memory_space=pltpu.HBM)
    operands = (
        top_list,
        leaf_list,
        jnp.transpose(send_index, (0, 2, 1)),
        rhs_block,
        leaf_basis,
        local_transfer,
        top_transfer,
        coupling_tiles,
    )
    dma = pltpu.SemaphoreType.DMA
    room = 40 if nleaf <= 16 else 60
    return pl.pallas_call(
        functools.partial(kernel, nleaf),
        out_shape=jax.ShapeDtypeStruct((width, npts), BF16),
        in_specs=[hbm] * len(operands),
        out_specs=vmem,
        scratch_shapes=[
            pltpu.VMEM((width, npts), BF16),
            pltpu.VMEM(leaf_basis.shape, BF16),
            pltpu.VMEM(local_transfer.shape[1:], BF16),
            pltpu.VMEM(top_transfer.shape, BF16),
            pltpu.VMEM((ntiles, rank, rank), BF16),
            pltpu.VMEM((leaves, width, rank), BF16),
            pltpu.VMEM((nleaf, slots * width, rank), BF16),
            pltpu.VMEM((nleaf, slots * width, rank), BF16),
            pltpu.VMEM((2 * nleaf, width, rank), BF16),
            pltpu.VMEM((width, rank), BF16),
            pltpu.VMEM((ntiles, leaves, pool_rows), F32),
            pltpu.VMEM((ntiles * leaves, pool_rows), BF16),
            pltpu.VMEM((width, pool_rows, rank), F32),
            pltpu.VMEM((ntiles // GROUP, width, leaves, GROUP * rank), BF16),
            pltpu.VMEM((width, leaves, rank), F32),
            pltpu.SMEM((slots, nleaf), jnp.int32),
            pltpu.VMEM((leaves, rank, rank), BF16),
            pltpu.SMEM(top_list.shape, jnp.int32),
            pltpu.VMEM(leaf_list.shape, jnp.int32),
            dma((7,)),
            dma,
            dma,
            dma,
            dma((chunks,)),
            dma((chunks,)),
            dma((chunks,)),
            dma((chunks,)),
            dma((chunks,)),
            dma((chunks,)),
            dma((nleaf, len(CUTS) - 1)),
            dma((nleaf, len(CUTS) - 1)),
            dma((nleaf,)),
            dma((nleaf,)),
        ],
        compiler_params=pltpu.CompilerParams(
            collective_id=0, has_side_effects=True, vmem_limit_bytes=room * 1024 * 1024
        ),
        name="far_field",
    )(*(pltpu.with_memory_space_constraint(a, pltpu.HBM) for a in operands))


def solution(mesh):
    placed = (
        P("rhs", "leaf"),
        P("leaf", None),
        P("leaf", None, None, None),
        P(),
        P("rhs", None, None),
        P(),
        P(None, "leaf", None),
        P(),
    )
    body = functools.partial(shards, mesh.shape["leaf"], mesh.shape["rhs"])
    return jax.shard_map(
        body, mesh=mesh, in_specs=placed, out_specs=P("rhs", "leaf"), check_vma=False
    )
```

```python
import functools

import jax
import jax.numpy as jnp
from jax import lax
from jax.experimental import pallas as pl
from jax.experimental.pallas import tpu as pltpu
from jax.sharding import PartitionSpec as P

F32 = jnp.float32
BF16 = jnp.bfloat16
MESH = pl.DeviceIdType.MESH
GROUP = 4
CHUNK = 2
CUTS = (0, 1, 3, 5, 7, 8)


def dot(a, b):
    return jnp.dot(a, b, preferred_element_type=F32)


def dot_nt(a, b):
    return lax.dot_general(a, b, (((1,), (1,)), ((), ())), preferred_element_type=F32)


def kernel(
    nleaf,
    tlist_hbm,
    llist_hbm,
    send_hbm,
    rhs_hbm,
    basis_hbm,
    local_hbm,
    top_hbm,
    tiles_hbm,
    out_ref,
    rhs,
    basis,
    local,
    top,
    table,
    xleaf,
    send,
    recv,
    xtop,
    xroot,
    tally_f,
    tally,
    pool,
    summed,
    acc,
    picks,
    down,
    top_list,
    leaf_list,
    in_sem,
    own_sem,
    part_send,
    part_recv,
    far_send,
    far_recv,
    side_send,
    side_recv,
    fwd_send,
    fwd_recv,
    pan_send,
    pan_recv,
    root_send,
    root_recv,
):
    me = lax.axis_index("leaf")
    mr = lax.axis_index("rhs")
    leaves, entries = leaf_list.shape[1:]
    slots = picks.shape[0]
    width = rhs.shape[0]
    rank = basis.shape[1]
    points = basis.shape[0] // leaves
    ntl = tiles_hbm.shape[0]
    ntiles = table.shape[0]
    groups = ntl // GROUP
    chunks = ntl // CHUNK
    pool_rows = nleaf * slots
    ltop = nleaf.bit_length() - 1
    cuts = [width * c // 8 for c in CUTS]
    parts = len(cuts) - 1

    barrier = pltpu.get_barrier_semaphore()
    for i in (1, 2):
        pl.semaphore_signal(barrier, inc=1, device_id={"rhs": mr ^ i}, device_id_type=MESH)
    for i in range(1, nleaf):
        pl.semaphore_signal(barrier, inc=1, device_id={"leaf": me ^ i}, device_id_type=MESH)

    loads = [
        pltpu.make_async_copy(src, dst, in_sem.at[i])
        for i, (src, dst) in enumerate(
            (
                (rhs_hbm, rhs),
                (basis_hbm, basis),
                (local_hbm.at[0], local),
                (top_hbm, top),
                (send_hbm.at[me], picks),
                (llist_hbm, leaf_list),
                (tlist_hbm, top_list),
            )
        )
    ]
    for i in (4, 0, 1, 2, 5, 6, 3):
        loads[i].start()
    own = pltpu.make_async_copy(tiles_hbm, table.at[pl.ds(mr * ntl, ntl)], own_sem)
    own.start()

    side = lax.rem(me, 2)
    borrowed = 2
    direct = chunks - borrowed - 1
    bit = lax.rem(lax.div(me, 2), 2)

    def rows_of(j, flip, turn):
        at = j + (side ^ flip) * (chunks - 1 - 2 * j) + (bit ^ turn) * (chunks // 2)
        at = lax.rem(at, chunks) * CHUNK
        return at, table.at[pl.ds((mr ^ 2) * ntl + at, CHUNK)]

    def far_copy(j):
        at, _ = rows_of(j, 0, 0)
        return pltpu.make_async_remote_copy(
            src_ref=tiles_hbm.at[pl.ds(at, CHUNK)],
            dst_ref=table.at[pl.ds(mr * ntl + at, CHUNK)],
            send_sem=far_send.at[j],
            recv_sem=far_recv.at[j],
            device_id={"rhs": mr ^ 2},
            device_id_type=MESH,
        )

    def side_copy(j):
        _, rows = rows_of(min(j, 1), 0, 0)
        return pltpu.make_async_remote_copy(
            src_ref=rows,
            dst_ref=rows,
            send_sem=side_send.at[j],
            recv_sem=side_recv.at[j],
            device_id={"leaf": me ^ (1 if j < borrowed else 2)},
            device_id_type=MESH,
        )

    def fwd_copy(k):
        if k < direct:
            _, rows = rows_of(k, 0, 0)
        elif k < direct + borrowed:
            _, rows = rows_of(k - direct, 1, 0)
        else:
            _, rows = rows_of(1, 0, 1)
        return pltpu.make_async_remote_copy(
            src_ref=rows,
            dst_ref=rows,
            send_sem=fwd_send.at[k],
            recv_sem=fwd_recv.at[k],
            device_id={"rhs": mr ^ 1},
            device_id_type=MESH,
        )

    far = [far_copy(j) for j in range(direct)]
    across = [side_copy(j) for j in range(borrowed + 1)]
    fwd = [fwd_copy(k) for k in range(chunks)]

    def pass_far(j):
        far[j].wait_recv()
        fwd[j].start()
        if j < borrowed:
            across[j].start()
        if j == 1:
            across[borrowed].start()

    def pass_across(j):
        across[j].wait_recv()
        fwd[direct + j].start()

    part = pltpu.make_async_remote_copy(
        src_ref=tiles_hbm,
        dst_ref=table.at[pl.ds(mr * ntl, ntl)],
        send_sem=part_send,
        recv_sem=part_recv,
        device_id={"rhs": mr ^ 1},
        device_id_type=MESH,
    )
    pl.semaphore_wait(barrier, nleaf + 1)
    for copy in far:
        copy.start()
    part.start()

    loads[4].wait()
    loads[0].wait()
    loads[1].wait()
    for g in range(leaves):
        cols = pl.ds(g * points, points)
        xleaf[g] = dot(rhs[:, cols], basis[cols, :]).astype(BF16)

    panels = [
        [
            pltpu.make_async_remote_copy(
                src_ref=send.at[i, pl.ds(cuts[q] * slots, (cuts[q + 1] - cuts[q]) * slots)],
                dst_ref=recv.at[i, pl.ds(cuts[q] * slots, (cuts[q + 1] - cuts[q]) * slots)],
                send_sem=pan_send.at[i, q],
                recv_sem=pan_recv.at[i, q],
                device_id={"leaf": me ^ i},
                device_id_type=MESH,
            )
            for i in range(1, nleaf)
        ]
        for q in range(parts)
    ]
    def fill(q):
        lo, hi = cuts[q], cuts[q + 1]
        for i in range(1, nleaf):
            for c in range(slots):
                pick = jnp.maximum(picks[c, me ^ i], 0)
                at = lo * slots + c * (hi - lo)
                send[i, at : at + hi - lo] = xleaf[pick, lo:hi]
            panels[q][i - 1].start() if q == 0 else None

    for q in range(parts):
        fill(q)

    loads[2].wait()
    level = [xleaf[g] for g in range(leaves)]
    count = leaves
    while count > 1:
        level = [
            (
                dot(level[2 * h], local[count - 2 + 2 * h])
                + dot(level[2 * h + 1], local[count - 1 + 2 * h])
            ).astype(BF16)
            for h in range(count // 2)
        ]
        count //= 2
    xroot[...] = level[0]
    roots = []
    for i in range(2, nleaf - 1):
        copy = pltpu.make_async_remote_copy(
            src_ref=xroot,
            dst_ref=xtop.at[nleaf + me],
            send_sem=root_send.at[i],
            recv_sem=root_recv.at[i],
            device_id={"leaf": lax.rem(me + i, nleaf)},
            device_id_type=MESH,
        )
        copy.start()
        roots.append(copy)
    for copy in panels[1]:
        copy.start()
    for n in range(4):
        xtop[n] = jnp.zeros((width, rank), BF16)
    for i in (0, 1, nleaf - 1):
        xtop[nleaf + lax.rem(me + i, nleaf)] = jnp.zeros((width, rank), BF16)

    loads[5].wait()
    tile_ids = lax.broadcasted_iota(jnp.int32, (ntiles, entries), 0)
    slot_ids = lax.broadcasted_iota(jnp.int32, (pool_rows, entries), 0)
    for g in range(leaves):
        here = leaf_list[0, g : g + 1, :] ^ (me * slots)
        tile = leaf_list[1, g : g + 1, :]
        tile_hot = jnp.where(tile_ids == tile, 1.0, 0.0).astype(BF16)
        slot_hot = jnp.where(slot_ids == here, 1.0, 0.0).astype(BF16)
        tally_f[:, g, :] = dot_nt(tile_hot, slot_hot)
    tally[...] = tally_f[...].reshape(ntiles * leaves, pool_rows).astype(BF16)

    mats = []
    for h in range(2 * leaves - 2):
        step = local[h]
        mats.append(dot(step, mats[h // 2 - 1]).astype(BF16) if h >= 2 else step)
        if h >= leaves - 2:
            down[h - leaves + 2] = mats[h]

    for c in range(slots):
        pick = jnp.maximum(picks[c, me], 0)
        pool[:, c, :] = xleaf[pick].astype(F32)

    rows_per = 16 * leaves

    def tally_step(bp, carry):
        weights = jnp.concatenate([pool[2 * bp], pool[2 * bp + 1]], axis=1).astype(BF16)
        for m in range(ntiles // 16):
            res = dot(tally[m * rows_per : (m + 1) * rows_per, :], weights)
            res = res.astype(BF16).reshape(16 // GROUP, GROUP, leaves, 2 * rank)
            q = pl.ds(m * (16 // GROUP), 16 // GROUP)
            for k in range(GROUP):
                for b in range(2):
                    summed[q, 2 * bp + b, :, k * rank : (k + 1) * rank] = res[
                        :, k, :, b * rank : (b + 1) * rank
                    ]
        return carry

    def couple(picked, q):
        lo, hi = cuts[q], cuts[q + 1]
        total = None
        for k in picked:
            lhs = summed[k, lo:hi].reshape((hi - lo) * leaves, GROUP * rank)
            res = dot(lhs, table[pl.ds(k * GROUP, GROUP)].reshape(GROUP * rank, rank))
            total = res if total is None else total + res
        return total.reshape(hi - lo, leaves, rank)

    def gather(q):
        lo, hi = cuts[q], cuts[q + 1]
        for copy in panels[q]:
            copy.wait_send()
        if q + 2 < parts:
            for copy in panels[q + 2]:
                copy.start()
        for i in range(1, nleaf):
            panels[q][i - 1].wait_recv()
            for c in range(slots):
                at = lo * slots + c * (hi - lo)
                pool[lo:hi, i * slots + c, :] = recv[i, at : at + hi - lo].astype(F32)
        lax.fori_loop(lo // 2, hi // 2, tally_step, 0, unroll=4)

    half = lax.div(mr, 2)
    near = [half * (2 * groups) + c for c in range(2 * groups)]
    away = [(1 - half) * (2 * groups) + c for c in range(2 * groups)]
    for j in range(3):
        pass_far(j)
    own.wait()
    part.wait_recv()
    early = 2
    for q in range(early):
        gather(q)
        acc[cuts[q] : cuts[q + 1]] = couple(near, q)
        if q == 0:
            for j in range(3, direct):
                pass_far(j)
    for j in range(borrowed + 1):
        pass_across(j)

    for copy in roots:
        copy.wait_recv()
    loads[3].wait()
    loads[6].wait()
    for lev in range(ltop - 1, 1, -1):
        for n in range(2**lev, 2 ** (lev + 1)):
            both = dot(xtop[2 * n], top[2 * n - 8]) + dot(xtop[2 * n + 1], top[2 * n - 7])
            xtop[n] = both.astype(BF16)

    gather(early)
    for copy in fwd:
        copy.wait_recv()
    for q in range(early):
        acc[cuts[q] : cuts[q + 1]] = acc[cuts[q] : cuts[q + 1]] + couple(away, q)
    acc[cuts[early] : cuts[early + 1]] = couple(near + away, early)

    node = nleaf + me
    depth = ltop - 1

    batch = 8

    def top_step(e, total):
        lhs = [[] for _ in range(depth)]
        rhs_mats = []
        for k in range(batch):
            at = e * batch + k
            target = top_list[0, at]
            x = xtop[top_list[1, at]].astype(F32)
            rhs_mats.append(table[top_list[2, at]])
            for j in range(depth):
                keep = jnp.where(target == lax.shift_right_logical(node, j), 1.0, 0.0)
                lhs[j].append((x * keep).astype(BF16))
        wide = jnp.concatenate([jnp.concatenate(row, axis=1) for row in lhs], axis=0)
        return total + dot(wide, jnp.concatenate(rhs_mats, axis=0))

    zero = jnp.zeros((depth * width, rank), F32)
    total = lax.fori_loop(0, top_list.shape[1] // batch, top_step, zero, unroll=8)
    ys = [total[j * width : (j + 1) * width] for j in range(depth)]
    y = ys[depth - 1]
    for j in range(depth - 2, -1, -1):
        y = ys[j] + dot_nt(y.astype(BF16), top[lax.shift_right_logical(node, j) - 8])

    y = y.astype(BF16)
    for q in range(early + 1, parts):
        gather(q)
        acc[cuts[q] : cuts[q + 1]] = couple(near + away, q)
    for g in range(leaves):
        wleaf = (acc[:, g, :] + dot_nt(y, down[g])).astype(BF16)
        cols = pl.ds(g * points, points)
        out_ref[:, cols] = dot_nt(wleaf, basis[cols, :]).astype(BF16)

    part.wait_send()
    for copy in far + across + fwd + roots:
        copy.wait_send()


def shards(
    nleaf,
    nrhs,
    rhs_block,
    leaf_basis,
    local_transfer,
    top_transfer,
    coupling_tiles,
    send_index,
    leaf_list,
    top_list,
):
    leaves = leaf_list.shape[1]
    width, npts = rhs_block.shape
    rank = leaf_basis.shape[1]
    slots = send_index.shape[2]
    ntl = coupling_tiles.shape[0]
    ntiles = ntl * nrhs
    pool_rows = nleaf * slots
    chunks = ntl // CHUNK
    vmem = pl.BlockSpec(memory_space=pltpu.VMEM)
    hbm = pl.BlockSpec(memory_space=pltpu.HBM)
    operands = (
        top_list,
        leaf_list,
        jnp.transpose(send_index, (0, 2, 1)),
        rhs_block,
        leaf_basis,
        local_transfer,
        top_transfer,
        coupling_tiles,
    )
    dma = pltpu.SemaphoreType.DMA
    room = 40 if nleaf <= 16 else 60
    return pl.pallas_call(
        functools.partial(kernel, nleaf),
        out_shape=jax.ShapeDtypeStruct((width, npts), BF16),
        in_specs=[hbm] * len(operands),
        out_specs=vmem,
        scratch_shapes=[
            pltpu.VMEM((width, npts), BF16),
            pltpu.VMEM(leaf_basis.shape, BF16),
            pltpu.VMEM(local_transfer.shape[1:], BF16),
            pltpu.VMEM(top_transfer.shape, BF16),
            pltpu.VMEM((ntiles, rank, rank), BF16),
            pltpu.VMEM((leaves, width, rank), BF16),
            pltpu.VMEM((nleaf, slots * width, rank), BF16),
            pltpu.VMEM((nleaf, slots * width, rank), BF16),
            pltpu.VMEM((2 * nleaf, width, rank), BF16),
            pltpu.VMEM((width, rank), BF16),
            pltpu.VMEM((ntiles, leaves, pool_rows), F32),
            pltpu.VMEM((ntiles * leaves, pool_rows), BF16),
            pltpu.VMEM((width, pool_rows, rank), F32),
            pltpu.VMEM((ntiles // GROUP, width, leaves, GROUP * rank), BF16),
            pltpu.VMEM((width, leaves, rank), F32),
            pltpu.SMEM((slots, nleaf), jnp.int32),
            pltpu.VMEM((leaves, rank, rank), BF16),
            pltpu.SMEM(top_list.shape, jnp.int32),
            pltpu.VMEM(leaf_list.shape, jnp.int32),
            dma((7,)),
            dma,
            dma,
            dma,
            dma((chunks,)),
            dma((chunks,)),
            dma((chunks,)),
            dma((chunks,)),
            dma((chunks,)),
            dma((chunks,)),
            dma((nleaf, len(CUTS) - 1)),
            dma((nleaf, len(CUTS) - 1)),
            dma((nleaf,)),
            dma((nleaf,)),
        ],
        compiler_params=pltpu.CompilerParams(
            collective_id=0, has_side_effects=True, vmem_limit_bytes=room * 1024 * 1024
        ),
        name="far_field",
    )(*(pltpu.with_memory_space_constraint(a, pltpu.HBM) for a in operands))


def solution(mesh):
    placed = (
        P("rhs", "leaf"),
        P("leaf", None),
        P("leaf", None, None, None),
        P(),
        P("rhs", None, None),
        P(),
        P(None, "leaf", None),
        P(),
    )
    body = functools.partial(shards, mesh.shape["leaf"], mesh.shape["rhs"])
    return jax.shard_map(
        body, mesh=mesh, in_specs=placed, out_specs=P("rhs", "leaf"), check_vma=False
    )
```

```python
import functools

import jax
import jax.numpy as jnp
from jax import lax
from jax.experimental import pallas as pl
from jax.experimental.pallas import tpu as pltpu
from jax.sharding import PartitionSpec as P

F32 = jnp.float32
BF16 = jnp.bfloat16
MESH = pl.DeviceIdType.MESH
GROUP = 4
CHUNK = 2
CUTS = (0, 1, 3, 5, 7, 8)


def dot(a, b):
    return jnp.dot(a, b, preferred_element_type=F32)


def dot_nt(a, b):
    return lax.dot_general(a, b, (((1,), (1,)), ((), ())), preferred_element_type=F32)


def kernel(
    nleaf,
    tlist_hbm,
    llist_hbm,
    send_hbm,
    rhs_hbm,
    basis_hbm,
    local_hbm,
    top_hbm,
    tiles_hbm,
    out_ref,
    rhs,
    basis,
    local,
    top,
    table,
    xleaf,
    send,
    recv,
    xtop,
    xroot,
    tally_f,
    tally,
    pool,
    summed,
    acc,
    picks,
    down,
    top_list,
    leaf_list,
    in_sem,
    own_sem,
    part_send,
    part_recv,
    far_send,
    far_recv,
    side_send,
    side_recv,
    fwd_send,
    fwd_recv,
    pan_send,
    pan_recv,
    root_send,
    root_recv,
):
    me = lax.axis_index("leaf")
    mr = lax.axis_index("rhs")
    leaves, entries = leaf_list.shape[1:]
    slots = picks.shape[0]
    width = rhs.shape[0]
    rank = basis.shape[1]
    points = basis.shape[0] // leaves
    ntl = tiles_hbm.shape[0]
    ntiles = table.shape[0]
    groups = ntl // GROUP
    chunks = ntl // CHUNK
    pool_rows = nleaf * slots
    ltop = nleaf.bit_length() - 1
    cuts = [width * c // 8 for c in CUTS]
    parts = len(cuts) - 1

    barrier = pltpu.get_barrier_semaphore()
    for i in (1, 2):
        pl.semaphore_signal(barrier, inc=1, device_id={"rhs": mr ^ i}, device_id_type=MESH)
    for i in range(1, nleaf):
        pl.semaphore_signal(barrier, inc=1, device_id={"leaf": me ^ i}, device_id_type=MESH)

    loads = [
        pltpu.make_async_copy(src, dst, in_sem.at[i])
        for i, (src, dst) in enumerate(
            (
                (rhs_hbm, rhs),
                (basis_hbm, basis),
                (local_hbm.at[0], local),
                (top_hbm, top),
                (send_hbm.at[me], picks),
                (llist_hbm, leaf_list),
                (tlist_hbm, top_list),
            )
        )
    ]
    for i in (4, 0, 1, 2, 5, 6, 3):
        loads[i].start()
    own = pltpu.make_async_copy(tiles_hbm, table.at[pl.ds(mr * ntl, ntl)], own_sem)
    own.start()

    side = lax.rem(me, 2)
    borrowed = 2
    direct = chunks - borrowed - 1
    bit = lax.rem(lax.div(me, 2), 2)

    def rows_of(j, flip, turn):
        at = j + (side ^ flip) * (chunks - 1 - 2 * j) + (bit ^ turn) * (chunks // 2)
        at = lax.rem(at, chunks) * CHUNK
        return at, table.at[pl.ds((mr ^ 2) * ntl + at, CHUNK)]

    def far_copy(j):
        at, _ = rows_of(j, 0, 0)
        return pltpu.make_async_remote_copy(
            src_ref=tiles_hbm.at[pl.ds(at, CHUNK)],
            dst_ref=table.at[pl.ds(mr * ntl + at, CHUNK)],
            send_sem=far_send.at[j],
            recv_sem=far_recv.at[j],
            device_id={"rhs": mr ^ 2},
            device_id_type=MESH,
        )

    def side_copy(j):
        _, rows = rows_of(min(j, 1), 0, 0)
        return pltpu.make_async_remote_copy(
            src_ref=rows,
            dst_ref=rows,
            send_sem=side_send.at[j],
            recv_sem=side_recv.at[j],
            device_id={"leaf": me ^ (1 if j < borrowed else 2)},
            device_id_type=MESH,
        )

    def fwd_copy(k):
        if k < direct:
            _, rows = rows_of(k, 0, 0)
        elif k < direct + borrowed:
            _, rows = rows_of(k - direct, 1, 0)
        else:
            _, rows = rows_of(1, 0, 1)
        return pltpu.make_async_remote_copy(
            src_ref=rows,
            dst_ref=rows,
            send_sem=fwd_send.at[k],
            recv_sem=fwd_recv.at[k],
            device_id={"rhs": mr ^ 1},
            device_id_type=MESH,
        )

    far = [far_copy(j) for j in range(direct)]
    across = [side_copy(j) for j in range(borrowed + 1)]
    fwd = [fwd_copy(k) for k in range(chunks)]

    def pass_far(j):
        far[j].wait_recv()
        fwd[j].start()
        if j < borrowed:
            across[j].start()
        if j == 1:
            across[borrowed].start()

    def pass_across(j):
        across[j].wait_recv()
        fwd[direct + j].start()

    part = pltpu.make_async_remote_copy(
        src_ref=tiles_hbm,
        dst_ref=table.at[pl.ds(mr * ntl, ntl)],
        send_sem=part_send,
        recv_sem=part_recv,
        device_id={"rhs": mr ^ 1},
        device_id_type=MESH,
    )
    pl.semaphore_wait(barrier, nleaf + 1)
    for copy in far:
        copy.start()
    part.start()

    loads[4].wait()
    loads[0].wait()
    loads[1].wait()
    for g in range(leaves):
        cols = pl.ds(g * points, points)
        xleaf[g] = dot(rhs[:, cols], basis[cols, :]).astype(BF16)

    panels = [
        [
            pltpu.make_async_remote_copy(
                src_ref=send.at[i, pl.ds(cuts[q] * slots, (cuts[q + 1] - cuts[q]) * slots)],
                dst_ref=recv.at[i, pl.ds(cuts[q] * slots, (cuts[q + 1] - cuts[q]) * slots)],
                send_sem=pan_send.at[i, q],
                recv_sem=pan_recv.at[i, q],
                device_id={"leaf": me ^ i},
                device_id_type=MESH,
            )
            for i in range(1, nleaf)
        ]
        for q in range(parts)
    ]
    def fill(q):
        lo, hi = cuts[q], cuts[q + 1]
        for i in range(1, nleaf):
            for c in range(slots):
                pick = jnp.maximum(picks[c, me ^ i], 0)
                at = lo * slots + c * (hi - lo)
                send[i, at : at + hi - lo] = xleaf[pick, lo:hi]
            panels[q][i - 1].start() if q == 0 else None

    for q in range(parts):
        fill(q)
        if q == 1:
            for copy in panels[1]:
                copy.start()

    loads[2].wait()
    level = [xleaf[g] for g in range(leaves)]
    count = leaves
    while count > 1:
        level = [
            (
                dot(level[2 * h], local[count - 2 + 2 * h])
                + dot(level[2 * h + 1], local[count - 1 + 2 * h])
            ).astype(BF16)
            for h in range(count // 2)
        ]
        count //= 2
    xroot[...] = level[0]
    roots = []
    for i in range(2, nleaf - 1):
        copy = pltpu.make_async_remote_copy(
            src_ref=xroot,
            dst_ref=xtop.at[nleaf + me],
            send_sem=root_send.at[i],
            recv_sem=root_recv.at[i],
            device_id={"leaf": lax.rem(me + i, nleaf)},
            device_id_type=MESH,
        )
        copy.start()
        roots.append(copy)
    for n in range(4):
        xtop[n] = jnp.zeros((width, rank), BF16)
    for i in (0, 1, nleaf - 1):
        xtop[nleaf + lax.rem(me + i, nleaf)] = jnp.zeros((width, rank), BF16)

    loads[5].wait()
    tile_ids = lax.broadcasted_iota(jnp.int32, (ntiles, entries), 0)
    slot_ids = lax.broadcasted_iota(jnp.int32, (pool_rows, entries), 0)
    for g in range(leaves):
        here = leaf_list[0, g : g + 1, :] ^ (me * slots)
        tile = leaf_list[1, g : g + 1, :]
        tile_hot = jnp.where(tile_ids == tile, 1.0, 0.0).astype(BF16)
        slot_hot = jnp.where(slot_ids == here, 1.0, 0.0).astype(BF16)
        tally_f[:, g, :] = dot_nt(tile_hot, slot_hot)
    tally[...] = tally_f[...].reshape(ntiles * leaves, pool_rows).astype(BF16)

    mats = []
    for h in range(2 * leaves - 2):
        step = local[h]
        mats.append(dot(step, mats[h // 2 - 1]).astype(BF16) if h >= 2 else step)
        if h >= leaves - 2:
            down[h - leaves + 2] = mats[h]

    for c in range(slots):
        pick = jnp.maximum(picks[c, me], 0)
        pool[:, c, :] = xleaf[pick].astype(F32)

    rows_per = 16 * leaves

    def tally_step(bp, carry):
        weights = jnp.concatenate([pool[2 * bp], pool[2 * bp + 1]], axis=1).astype(BF16)
        for m in range(ntiles // 16):
            res = dot(tally[m * rows_per : (m + 1) * rows_per, :], weights)
            res = res.astype(BF16).reshape(16 // GROUP, GROUP, leaves, 2 * rank)
            q = pl.ds(m * (16 // GROUP), 16 // GROUP)
            for k in range(GROUP):
                for b in range(2):
                    summed[q, 2 * bp + b, :, k * rank : (k + 1) * rank] = res[
                        :, k, :, b * rank : (b + 1) * rank
                    ]
        return carry

    def couple(picked, q):
        lo, hi = cuts[q], cuts[q + 1]
        total = None
        for k in picked:
            lhs = summed[k, lo:hi].reshape((hi - lo) * leaves, GROUP * rank)
            res = dot(lhs, table[pl.ds(k * GROUP, GROUP)].reshape(GROUP * rank, rank))
            total = res if total is None else total + res
        return total.reshape(hi - lo, leaves, rank)

    def gather(q):
        lo, hi = cuts[q], cuts[q + 1]
        for copy in panels[q]:
            copy.wait_send()
        if q + 2 < parts:
            for copy in panels[q + 2]:
                copy.start()
        for i in range(1, nleaf):
            panels[q][i - 1].wait_recv()
            for c in range(slots):
                at = lo * slots + c * (hi - lo)
                pool[lo:hi, i * slots + c, :] = recv[i, at : at + hi - lo].astype(F32)
        lax.fori_loop(lo // 2, hi // 2, tally_step, 0, unroll=8 if q == 3 else 4)

    half = lax.div(mr, 2)
    near = [half * (2 * groups) + c for c in range(2 * groups)]
    away = [(1 - half) * (2 * groups) + c for c in range(2 * groups)]
    for j in range(3):
        pass_far(j)
    own.wait()
    part.wait_recv()
    early = 2
    for q in range(early):
        gather(q)
        acc[cuts[q] : cuts[q + 1]] = couple(near, q)
        if q == 0:
            for j in range(3, direct):
                pass_far(j)
    for j in range(borrowed + 1):
        pass_across(j)

    for copy in roots:
        copy.wait_recv()
    loads[3].wait()
    loads[6].wait()
    for lev in range(ltop - 1, 1, -1):
        for n in range(2**lev, 2 ** (lev + 1)):
            both = dot(xtop[2 * n], top[2 * n - 8]) + dot(xtop[2 * n + 1], top[2 * n - 7])
            xtop[n] = both.astype(BF16)

    gather(early)
    for copy in fwd:
        copy.wait_recv()
    for q in range(early):
        acc[cuts[q] : cuts[q + 1]] = acc[cuts[q] : cuts[q + 1]] + couple(away, q)
    acc[cuts[early] : cuts[early + 1]] = couple(near + away, early)

    node = nleaf + me
    depth = ltop - 1

    batch = 8

    def top_step(e, total):
        lhs = [[] for _ in range(depth)]
        rhs_mats = []
        for k in range(batch):
            at = e * batch + k
            target = top_list[0, at]
            x = xtop[top_list[1, at]].astype(F32)
            rhs_mats.append(table[top_list[2, at]])
            for j in range(depth):
                keep = jnp.where(target == lax.shift_right_logical(node, j), 1.0, 0.0)
                lhs[j].append((x * keep).astype(BF16))
        wide = jnp.concatenate([jnp.concatenate(row, axis=1) for row in lhs], axis=0)
        return total + dot(wide, jnp.concatenate(rhs_mats, axis=0))

    zero = jnp.zeros((depth * width, rank), F32)
    total = lax.fori_loop(0, top_list.shape[1] // batch, top_step, zero, unroll=8)
    ys = [total[j * width : (j + 1) * width] for j in range(depth)]
    y = ys[depth - 1]
    for j in range(depth - 2, -1, -1):
        y = ys[j] + dot_nt(y.astype(BF16), top[lax.shift_right_logical(node, j) - 8])

    y = y.astype(BF16)
    for q in range(early + 1, parts):
        gather(q)
        acc[cuts[q] : cuts[q + 1]] = couple(near + away, q)
    for g in range(leaves):
        wleaf = (acc[:, g, :] + dot_nt(y, down[g])).astype(BF16)
        cols = pl.ds(g * points, points)
        out_ref[:, cols] = dot_nt(wleaf, basis[cols, :]).astype(BF16)

    part.wait_send()
    for copy in far + across + fwd + roots:
        copy.wait_send()


def shards(
    nleaf,
    nrhs,
    rhs_block,
    leaf_basis,
    local_transfer,
    top_transfer,
    coupling_tiles,
    send_index,
    leaf_list,
    top_list,
):
    leaves = leaf_list.shape[1]
    width, npts = rhs_block.shape
    rank = leaf_basis.shape[1]
    slots = send_index.shape[2]
    ntl = coupling_tiles.shape[0]
    ntiles = ntl * nrhs
    pool_rows = nleaf * slots
    chunks = ntl // CHUNK
    vmem = pl.BlockSpec(memory_space=pltpu.VMEM)
    hbm = pl.BlockSpec(memory_space=pltpu.HBM)
    operands = (
        top_list,
        leaf_list,
        jnp.transpose(send_index, (0, 2, 1)),
        rhs_block,
        leaf_basis,
        local_transfer,
        top_transfer,
        coupling_tiles,
    )
    dma = pltpu.SemaphoreType.DMA
    room = 40 if nleaf <= 16 else 60
    return pl.pallas_call(
        functools.partial(kernel, nleaf),
        out_shape=jax.ShapeDtypeStruct((width, npts), BF16),
        in_specs=[hbm] * len(operands),
        out_specs=vmem,
        scratch_shapes=[
            pltpu.VMEM((width, npts), BF16),
            pltpu.VMEM(leaf_basis.shape, BF16),
            pltpu.VMEM(local_transfer.shape[1:], BF16),
            pltpu.VMEM(top_transfer.shape, BF16),
            pltpu.VMEM((ntiles, rank, rank), BF16),
            pltpu.VMEM((leaves, width, rank), BF16),
            pltpu.VMEM((nleaf, slots * width, rank), BF16),
            pltpu.VMEM((nleaf, slots * width, rank), BF16),
            pltpu.VMEM((2 * nleaf, width, rank), BF16),
            pltpu.VMEM((width, rank), BF16),
            pltpu.VMEM((ntiles, leaves, pool_rows), F32),
            pltpu.VMEM((ntiles * leaves, pool_rows), BF16),
            pltpu.VMEM((width, pool_rows, rank), F32),
            pltpu.VMEM((ntiles // GROUP, width, leaves, GROUP * rank), BF16),
            pltpu.VMEM((width, leaves, rank), F32),
            pltpu.SMEM((slots, nleaf), jnp.int32),
            pltpu.VMEM((leaves, rank, rank), BF16),
            pltpu.SMEM(top_list.shape, jnp.int32),
            pltpu.VMEM(leaf_list.shape, jnp.int32),
            dma((7,)),
            dma,
            dma,
            dma,
            dma((chunks,)),
            dma((chunks,)),
            dma((chunks,)),
            dma((chunks,)),
            dma((chunks,)),
            dma((chunks,)),
            dma((nleaf, len(CUTS) - 1)),
            dma((nleaf, len(CUTS) - 1)),
            dma((nleaf,)),
            dma((nleaf,)),
        ],
        compiler_params=pltpu.CompilerParams(
            collective_id=0, has_side_effects=True, vmem_limit_bytes=room * 1024 * 1024
        ),
        name="far_field",
    )(*(pltpu.with_memory_space_constraint(a, pltpu.HBM) for a in operands))


def solution(mesh):
    placed = (
        P("rhs", "leaf"),
        P("leaf", None),
        P("leaf", None, None, None),
        P(),
        P("rhs", None, None),
        P(),
        P(None, "leaf", None),
        P(),
    )
    body = functools.partial(shards, mesh.shape["leaf"], mesh.shape["rhs"])
    return jax.shard_map(
        body, mesh=mesh, in_specs=placed, out_specs=P("rhs", "leaf"), check_vma=False
    )
```
